512 devices in a mesh: row: 16 (over y, z_hi), col: 32 (over x, z_lo, core).
Axes of the slice: x: 4, y: 4, z: 16 (z_hi: 4, z_lo: 4; z = z_hi * 4 + z_lo), core: 2. Of those that a mesh axis runs over, the one named last changes fastest.
Arguments:
- nodes: bfloat16 [1024, 768], P('col'), may hold values from -6 to 6
- node_gain: float32 [768], replicated, may hold values from 0.25 to 1.75
- w_qkv: bfloat16 [3, 768, 768], P(None, None, 'row'), may hold values from -0.21875 to 0.21875
- w_out: bfloat16 [768, 768], P(None, 'col'), may hold values from -0.4375 to 0.4375
- pair: bfloat16 [1024, 1024, 128], P('row', 'col'), may hold values from -16 to 16
- pair_gain: float32 [128], replicated, may hold values from 0.25 to 1.75
- w_bias: bfloat16 [128, 16], replicated, may hold values from -10 to 10, as said below
- w_gate: bfloat16 [128, 16], replicated, may hold values from -0.5 to 0.5
- b_gate: float32 [16], replicated, may hold values from -1 to 3
- w_in: bfloat16 [256, 512], replicated, may hold values from -0.375 to 0.375
- b_in: float32 [512], replicated, may hold values from -3 to 3
- w_mlp_out: bfloat16 [512, 128], replicated, may hold values from -0.25 to 0.25
- b_out: float32 [128], replicated, may hold values from -3 to 3
Outputs:
- node_update: bfloat16 [1024, 768], P('row', 'col')
- pair_out: bfloat16 [1024, 1024, 128], P('row', 'col')
The draws below stay inside these ranges and needn't reach their ends.
Inputs may be any that keep to these rules, and one draw needn't show every extreme that they name: `w_bias`: entries are of order 2.2 / sqrt(128).
All inputs are finite; a program needn't handle non-finite values.
Results may differ from the reference program's by a relative error of at most 0.011.
Values may be sent and summed in bfloat16 or wider, within the bound.
No kernel may reach another device: no remote copies, remote signals or barrier semaphores. Data moves between devices by JAX's collectives and lax.ppermute only.
A program may use at most 64 MiB of HBM per device.

```python
import math
import jax
import jax.numpy as jnp
from jax import lax

D = 768
H = 16
C = 128
FFE = 512
ROW_NODES = 64
NODES = 1024
N_ROW = 16


def shared_bias(key):
    raw_bias = jax.random.normal(jax.random.fold_in(key, 7), (C, H), jnp.float32)
    return jnp.clip(raw_bias, -4.5, 4.5) * (2.2 / math.sqrt(C))


def draw_w_bias(key, part):
    return shared_bias(key).astype(jnp.bfloat16)


def draw_pair(key, part):
    values_base = jnp.clip(jax.random.normal(jax.random.fold_in(key, 11), (NODES, NODES, C), jnp.float32), -6.0, 6.0)
    return values_base.astype(jnp.bfloat16)


def block_levels(key, extent, split, low, high):
    gain, own = 1.0, jax.random.fold_in(key, 6)
    for axis_at, shards_of in split:
        steps = jnp.exp(jax.random.uniform(jax.random.fold_in(own, axis_at), (shards_of,), jnp.float32, low / len(split), high / len(split)))
        gain = gain * jnp.repeat(steps, extent[axis_at] // shards_of).reshape([-1 if axis == axis_at else 1 for axis in range(len(extent))])
    return gain


def bell_draw(key, shape, width, limit, split=(), kind=jnp.bfloat16):
    gain = block_levels(key, shape, split, -0.22, 0.18) if split else 1.0
    entries = jax.random.normal(key, shape, jnp.float32) * width * gain
    return jnp.minimum(jnp.maximum(entries, -limit), limit).astype(kind)


def setup_inputs(seed: int = 0) -> dict:
    splits = jax.random.split(jax.random.key(seed), 14)
    return {
        "nodes": bell_draw(splits[0], (NODES, D), 1.0, 6.0, ((0, 32),)),
        "node_gain": jnp.clip(1.0 + 0.15 * jax.random.normal(splits[1], (D,), jnp.float32), 0.25, 1.75),
        "w_qkv": bell_draw(splits[2], (3, D, D), D ** -0.5, 0.21875, ((2, 16),)),
        "w_out": bell_draw(splits[3], (D, D), (D // 4) ** -0.5, 0.4375, ((1, 32),)),
        "pair": draw_pair(jax.random.fold_in(splits[13], 71), 0),
        "pair_gain": jnp.clip(1.0 + 0.15 * jax.random.normal(splits[5], (C,), jnp.float32), 0.25, 1.75),
        "w_bias": draw_w_bias(jax.random.fold_in(splits[13], 71), 0),
        "w_gate": bell_draw(splits[7], (C, H), C ** -0.5, 0.5),
        "b_gate": jnp.clip(jax.random.uniform(splits[8], (H,), jnp.float32, -1.0, 3.0), -1.0, 3.0),
        "w_in": bell_draw(splits[9], (2 * C, FFE), (2 * C) ** -0.5, 0.375),
        "b_in": bell_draw(splits[10], (FFE,), 0.5, 3.0, (), jnp.float32),
        "w_mlp_out": bell_draw(splits[11], (FFE, C), FFE ** -0.5, 0.25),
        "b_out": bell_draw(splits[12], (C,), 0.5, 3.0, (), jnp.float32),
    }


def layer_norm(values_in, scale_gain):
    centred = values_in.astype(jnp.float32)
    centred = centred - lax.optimization_barrier(jnp.mean(centred, axis=-1, keepdims=True))
    variance = lax.optimization_barrier(jnp.mean(centred * centred, axis=-1, keepdims=True))
    return centred * lax.rsqrt(variance + 1e-05) * scale_gain

def reference(nodes, node_gain, w_qkv, w_out, pair, pair_gain, w_bias, w_gate, b_gate, w_in, b_in, w_mlp_out, b_out):
    head_size = D // H
    normed = layer_norm(nodes, node_gain).astype(jnp.bfloat16)
    projected = jnp.stack([jnp.dot(normed, w_qkv[which], preferred_element_type=jnp.float32) for which in range(3)]).astype(jnp.bfloat16)
    key_heads = projected[1].astype(jnp.float32).reshape(NODES, H, head_size)
    value_heads = projected[2].astype(jnp.float32).reshape(NODES, H, head_size)

    def attend(row_start):
        row_piece = lax.dynamic_slice_in_dim(pair, row_start, ROW_NODES, 0)
        query_rows = lax.dynamic_slice_in_dim(projected[0], row_start, ROW_NODES, 0).astype(jnp.float32).reshape(ROW_NODES, H, head_size)
        scores = jnp.einsum('ihe,jhe->hij', query_rows, key_heads) / math.sqrt(head_size)
        pair_bias = jnp.einsum('ijc,ch->hij', row_piece.astype(jnp.float32), w_bias.astype(jnp.float32))
        zed = layer_norm(row_piece, pair_gain).astype(jnp.bfloat16)
        gate_prob = jax.nn.sigmoid(jnp.einsum('ijc,ch->hij', zed.astype(jnp.float32), w_gate.astype(jnp.float32)) + b_gate[:, None, None])
        logits = scores + pair_bias
        top_score = lax.optimization_barrier(jnp.max(logits, axis=2, keepdims=True))
        expo_score = jnp.exp(logits - top_score)
        denom_sum = lax.optimization_barrier(jnp.sum(expo_score, axis=2))
        weights = lax.optimization_barrier((expo_score * gate_prob).astype(jnp.bfloat16)).astype(jnp.float32)
        weighted_sum = jnp.einsum('hij,jhe->ihe', weights, value_heads)
        attended = (weighted_sum / denom_sum.T[:, :, None]).reshape(ROW_NODES, D).astype(jnp.bfloat16)
        return jnp.dot(attended, w_out, preferred_element_type=jnp.float32).astype(jnp.bfloat16)
    row_starts = (jnp.arange(N_ROW) * ROW_NODES).astype(jnp.int32)
    node_update = lax.map(attend, row_starts).reshape(NODES, D)

    def edge_mlp(row_start):
        row_piece = lax.dynamic_slice_in_dim(pair, row_start, 16, 0)
        reverse_tile = jnp.transpose(lax.dynamic_slice_in_dim(pair, row_start, 16, 1), (1, 0, 2))
        zed = layer_norm(row_piece, pair_gain).astype(jnp.bfloat16)
        zed_reverse = layer_norm(reverse_tile, pair_gain).astype(jnp.bfloat16)
        joined = jnp.concatenate([zed, zed_reverse], axis=-1).reshape(16 * NODES, 2 * C)
        hidden = jax.nn.gelu(jnp.dot(joined, w_in, preferred_element_type=jnp.float32) + b_in).astype(jnp.bfloat16)
        update = jnp.dot(hidden, w_mlp_out, preferred_element_type=jnp.float32) + b_out
        return (row_piece.astype(jnp.float32) + update.reshape(16, NODES, C)).astype(jnp.bfloat16)
    mlp_starts = (jnp.arange(NODES // 16) * 16).astype(jnp.int32)
    pair_out = lax.map(edge_mlp, mlp_starts).reshape(NODES, NODES, C)
    return (node_update, pair_out)
```

```python
import math

import jax
import jax.numpy as jnp
from jax import lax
from jax.sharding import PartitionSpec as P

F32 = jnp.float32
BF16 = jnp.bfloat16


def rounded(values):
    return lax.reduce_precision(values, 8, 7)


def layer_norm(values_in, scale_gain):
    centred = values_in.astype(F32)
    centred = centred - jnp.mean(centred, axis=-1, keepdims=True)
    variance = jnp.mean(centred * centred, axis=-1, keepdims=True)
    return centred * lax.rsqrt(variance + 1e-05) * scale_gain


def body(
    nodes,
    node_gain,
    w_qkv,
    w_out,
    pair,
    pair_gain,
    w_bias,
    w_gate,
    b_gate,
    w_in,
    b_in,
    w_mlp_out,
    b_out,
):
    rows_n = lax.axis_size("row")
    cols_n = lax.axis_size("col")
    key_rows, node_width = nodes.shape
    row_rows, key_cols, pair_width = pair.shape
    heads = w_bias.shape[1]
    head_size = node_width // heads
    half = key_rows // 2
    col = lax.axis_index("col")

    normed = layer_norm(nodes, node_gain).astype(BF16)
    proj = jnp.einsum("nd,kde->kne", normed, w_qkv, preferred_element_type=F32).astype(BF16)
    packed = jnp.concatenate([proj[:, :half], proj[:, half:]], axis=-1)
    spread = jnp.broadcast_to(packed[0][None], (cols_n,) + packed.shape[1:])
    all_q = lax.all_to_all(spread, "col", 0, 0, tiled=True)

    zed = layer_norm(pair, pair_gain).astype(BF16)
    zed_t = jnp.transpose(zed, (1, 0, 2))
    odd = col % 2
    first = lax.dynamic_slice_in_dim(zed_t, odd * key_cols, key_cols, 1)
    second = lax.dynamic_slice_in_dim(zed_t, (1 - odd) * key_cols, key_cols, 1)
    same = [
        (r * cols_n + c, (c // 2) * cols_n + 2 * r + c % 2)
        for r in range(rows_n)
        for c in range(cols_n)
    ]
    swap = [
        (r * cols_n + c, (c // 2) * cols_n + 2 * r + 1 - c % 2)
        for r in range(rows_n)
        for c in range(cols_n)
    ]
    back_one = lax.ppermute(first, ("row", "col"), same)
    back_two = lax.ppermute(second, ("row", "col"), swap)

    own_kv = jnp.concatenate([packed[1], packed[2]], axis=0)
    sent = jnp.concatenate(
        [
            all_q.reshape(rows_n, 2 * half, 2 * head_size),
            jnp.broadcast_to(own_kv[None], (rows_n,) + own_kv.shape),
        ],
        axis=1,
    )
    got = lax.all_to_all(sent, "row", 0, 0, tiled=True)

    def unpack(piece, blocks):
        piece = piece.reshape(heads, blocks, half, 2, head_size)
        return jnp.transpose(piece, (0, 1, 3, 2, 4)).reshape(heads, blocks * key_rows, head_size)

    query = unpack(got[:, : 2 * half], 2)
    key = unpack(got[:, 2 * half : 3 * half], 1)
    value = unpack(got[:, 3 * half :], 1)

    scores = jnp.einsum("hie,hje->hij", query, key, preferred_element_type=F32) / math.sqrt(head_size)
    pair_bias = jnp.einsum("ijc,ch->hij", pair, w_bias, preferred_element_type=F32)
    gate_prob = jax.nn.sigmoid(
        jnp.einsum("ijc,ch->hij", zed, w_gate, preferred_element_type=F32) + b_gate[:, None, None]
    )
    logits = scores + pair_bias
    peak = jnp.max(logits, axis=2)
    peak_hi = rounded(peak)
    peak_lo = rounded(peak - peak_hi)
    expo = jnp.exp(logits - (peak_hi + peak_lo)[:, :, None])
    denom = jnp.sum(expo, axis=2)
    weights = (expo * gate_prob).astype(BF16)
    part = jnp.einsum("hij,hje->ihe", weights, value, preferred_element_type=F32)
    denom_hi = rounded(denom)
    denom_lo = rounded(denom - denom_hi)
    stats = jnp.concatenate([peak_hi.T, peak_lo.T, denom_hi.T, denom_lo.T], axis=1)
    parcel = jnp.concatenate([part.reshape(row_rows, node_width), stats], axis=1).astype(BF16)
    share = row_rows // cols_n
    heard = lax.all_to_all(
        parcel.reshape(cols_n, share, parcel.shape[1]), "col", 0, 0, tiled=True
    ).astype(F32)
    tail = [
        heard[:, :, node_width + k * heads : node_width + (k + 1) * heads] for k in range(4)
    ]
    peaks = tail[0] + tail[1]
    factor = jnp.exp(peaks - jnp.max(peaks, axis=0, keepdims=True))
    total = jnp.sum(factor * (tail[2] + tail[3]), axis=0)
    mixed = jnp.sum(
        heard[:, :, :node_width].reshape(cols_n, share, heads, head_size) * factor[..., None], axis=0
    )
    attended = (mixed / total[..., None]).reshape(share, node_width).astype(BF16)
    everyone = lax.all_to_all(
        jnp.broadcast_to(attended[None], (cols_n,) + attended.shape), "col", 0, 0, tiled=True
    )
    node_update = jnp.dot(
        everyone.reshape(row_rows, node_width), w_out, preferred_element_type=F32
    ).astype(BF16)

    def edge_mlp(start, zed_back):
        zed_here = lax.dynamic_slice_in_dim(zed, start, key_cols, 0)
        pair_here = lax.dynamic_slice_in_dim(pair, start, key_cols, 0)
        joined = jnp.concatenate([zed_here, zed_back], axis=-1).reshape(-1, 2 * pair_width)
        hidden = jax.nn.gelu(jnp.dot(joined, w_in, preferred_element_type=F32) + b_in).astype(BF16)
        update = jnp.dot(hidden, w_mlp_out, preferred_element_type=F32) + b_out
        return (pair_here.astype(F32) + update.reshape(pair_here.shape)).astype(BF16)

    out = jnp.zeros(pair.shape, BF16)
    out = lax.dynamic_update_slice_in_dim(out, edge_mlp(odd * key_cols, back_one), odd * key_cols, 0)
    out = lax.dynamic_update_slice_in_dim(
        out, edge_mlp((1 - odd) * key_cols, back_two), (1 - odd) * key_cols, 0
    )
    return (node_update, out)


def solution(mesh):
    return jax.shard_map(
        body,
        mesh=mesh,
        in_specs=(
            P("col", None),
            P(),
            P(None, None, "row"),
            P(None, "col"),
            P("row", "col", None),
            P(),
            P(),
            P(),
            P(),
            P(),
            P(),
            P(),
            P(),
        ),
        out_specs=(P("row", "col"), P("row", "col", None)),
        check_vma=False,
    )
```

```python
import math

import jax
import jax.numpy as jnp
from jax import lax
from jax.sharding import PartitionSpec as P

F32 = jnp.float32
BF16 = jnp.bfloat16
PLAN = [('a', 0, 2, 'att'), ('a', 1, 2, 'att'), ('b', 0, 2, 'att'), ('b', 1, 2, 'end')]
LONG = ("row", "col")


def tie(value, *others):
    return lax.optimization_barrier((value,) + others)[0]


def rounded(values):
    return lax.reduce_precision(values, 8, 7)


def layer_norm(values_in, scale_gain):
    centred = values_in.astype(F32)
    centred = centred - jnp.mean(centred, axis=-1, keepdims=True)
    variance = jnp.mean(centred * centred, axis=-1, keepdims=True)
    return centred * lax.rsqrt(variance + 1e-05) * scale_gain


def body(
    nodes, node_gain, w_qkv, w_out, pair, pair_gain, w_bias, w_gate, b_gate, w_in, b_in, w_mlp_out, b_out,
):
    rows_n = lax.axis_size("row")
    cols_n = lax.axis_size("col")
    key_rows, node_width = nodes.shape
    row_rows, key_cols, pair_width = pair.shape
    heads = w_bias.shape[1]
    head_size = node_width // heads
    half = key_rows // 2
    col = lax.axis_index("col")
    odd = col % 2
    same = [
        (r * cols_n + c, (c // 2) * cols_n + 2 * r + c % 2) for r in range(rows_n) for c in range(cols_n)
    ]
    swap = [
        (r * cols_n + c, (c // 2) * cols_n + 2 * r + 1 - c % 2) for r in range(rows_n) for c in range(cols_n)
    ]

    zed = layer_norm(pair, pair_gain).astype(BF16)
    landed = []
    for which, part, parts, late in PLAN:
        own = odd if which == "a" else 1 - odd
        rows = key_cols // parts
        tile = lax.dynamic_slice_in_dim(zed, own * key_cols, key_cols, 0)[:, part * rows : (part + 1) * rows]
        landed.append(
            (lax.ppermute(jnp.transpose(tile, (1, 0, 2)), LONG, same if which == "a" else swap), own * key_cols + part * rows, late)
        )
    normed = layer_norm(nodes, node_gain).astype(BF16)
    proj = jnp.einsum("nd,kde->kne", normed, w_qkv, preferred_element_type=F32).astype(BF16)
    packed = jnp.concatenate([proj[:, :half], proj[:, half:]], axis=-1)
    spread = jnp.broadcast_to(packed[0][None], (cols_n,) + packed.shape[1:])
    all_q = lax.all_to_all(spread, "col", 0, 0, tiled=True)
    blocks = all_q.reshape(rows_n, 2, half, 2 * head_size)
    own = [jnp.broadcast_to(packed[k][None], (rows_n,) + packed.shape[1:]) for k in (1, 2)]
    sent = jnp.concatenate([blocks[:, 0], blocks[:, 1]] + own, axis=-1)
    got = lax.all_to_all(sent, "row", 0, 0, tiled=True)

    def unpack(piece):
        chunks = piece.shape[2] // head_size
        piece = piece.reshape(heads, half, chunks, head_size)
        return jnp.transpose(piece, (0, 2, 1, 3)).reshape(heads, chunks * half, head_size)

    width = 2 * head_size
    query = unpack(got[:, :, : 2 * width])
    key = unpack(got[:, :, 2 * width : 3 * width])
    value = unpack(got[:, :, 3 * width :])

    scores = jnp.einsum("hie,hje->hij", query, key, preferred_element_type=F32) / math.sqrt(head_size)
    pair_bias = jnp.einsum("ijc,ch->hij", pair, w_bias, preferred_element_type=F32)
    gate_prob = jax.nn.sigmoid(
        jnp.einsum("ijc,ch->hij", zed, w_gate, preferred_element_type=F32) + b_gate[:, None, None]
    )
    logits = scores + pair_bias
    peak = jnp.max(logits, axis=2)
    peak_hi = rounded(peak)
    peak_lo = rounded(peak - peak_hi)
    expo = jnp.exp(logits - (peak_hi + peak_lo)[:, :, None])
    denom = jnp.sum(expo, axis=2)
    weights = (expo * gate_prob).astype(BF16)
    part = jnp.einsum("hij,hje->ihe", weights, value, preferred_element_type=F32)
    denom_hi = rounded(denom)
    denom_lo = rounded(denom - denom_hi)
    stats = jnp.concatenate([peak_hi.T, peak_lo.T, denom_hi.T, denom_lo.T], axis=1)
    parcel = jnp.concatenate([part.reshape(row_rows, node_width), stats], axis=1).astype(BF16)
    share = row_rows // cols_n
    heard = lax.all_to_all(parcel.reshape(cols_n, share, parcel.shape[1]), "col", 0, 0, tiled=True)
    heard = heard.astype(F32)
    tail = [heard[:, :, node_width + k * heads : node_width + (k + 1) * heads] for k in range(4)]
    peaks = tail[0] + tail[1]
    factor = jnp.exp(peaks - jnp.max(peaks, axis=0, keepdims=True))
    total = jnp.sum(factor * (tail[2] + tail[3]), axis=0)
    mixed = jnp.sum(
        heard[:, :, :node_width].reshape(cols_n, share, heads, head_size) * factor[..., None], axis=0
    )
    attended = (mixed / total[..., None]).reshape(share, node_width).astype(BF16)
    everyone = lax.all_to_all(
        jnp.broadcast_to(attended[None], (cols_n,) + attended.shape), "col", 0, 0, tiled=True
    )
    node_update = jnp.dot(
        everyone.reshape(row_rows, node_width), w_out, preferred_element_type=F32
    ).astype(BF16)

    def edge_mlp(start, zed_back):
        count = zed_back.shape[0]
        zed_here = lax.dynamic_slice_in_dim(zed, start, count, 0)
        pair_here = lax.dynamic_slice_in_dim(pair, start, count, 0)
        joined = jnp.concatenate([zed_here, zed_back], axis=-1).reshape(-1, 2 * pair_width)
        hidden = jax.nn.gelu(jnp.dot(joined, w_in, preferred_element_type=F32) + b_in).astype(BF16)
        update = jnp.dot(hidden, w_mlp_out, preferred_element_type=F32) + b_out
        return (pair_here.astype(F32) + update.reshape(pair_here.shape)).astype(BF16)

    out = jnp.zeros(pair.shape, BF16)
    for back, start, late in landed:
        back = tie(back, attended if late == "att" else everyone)
        out = lax.dynamic_update_slice_in_dim(out, edge_mlp(start, back), start, 0)
    return (node_update, out)


def solution(mesh):
    return jax.shard_map(
        body,
        mesh=mesh,
        in_specs=(
            P("col", None), P(), P(None, None, "row"), P(None, "col"), P("row", "col", None),
            P(), P(), P(), P(), P(), P(), P(), P(),
        ),
        out_specs=(P("row", "col"), P("row", "col", None)),
        check_vma=False,
    )
```

```python
import functools
import math

import jax
import jax.numpy as jnp
from jax import lax
from jax.experimental import pallas as pl
from jax.experimental.pallas import tpu as pltpu
from jax.sharding import PartitionSpec as P

F32 = jnp.float32
BF16 = jnp.bfloat16
LONG = ("row", "col")
LANES = 128
VMEM_BYTES = 20 << 20


def tie(value, *others):
    return lax.optimization_barrier((value,) + others)[0]


def layer_norm(values_in, scale_gain):
    centred = values_in.astype(F32)
    centred = centred - jnp.mean(centred, axis=-1, keepdims=True)
    variance = jnp.mean(centred * centred, axis=-1, keepdims=True)
    return centred * lax.rsqrt(variance + 1e-05) * scale_gain


def nt_dot(left, right):
    return lax.dot_general(left, right, (((1,), (1,)), ((), ())), preferred_element_type=F32)


def rounded(values):
    return values.astype(BF16).astype(F32)


def project_kernel(nodes_ref, gain_ref, w_ref, spread_ref, own_ref):
    normed = layer_norm(nodes_ref[...], gain_ref[...]).astype(BF16)
    half = normed.shape[0] // 2
    for which in range(3):
        proj = nt_dot(normed, w_ref[which])
        packed = jnp.concatenate([proj[:half], proj[half:]], axis=-1).astype(BF16)
        if which == 0:
            spread_ref[...] = jnp.broadcast_to(packed[None], spread_ref.shape)
        else:
            own_ref[which - 1] = packed


def attend_kernel(got_ref, bias_ref, gate_ref, select_ref, parcel_ref, *, heads, size):
    half = got_ref.shape[1]
    pairs = heads // 2
    width = pairs * LANES
    got = got_ref[...].astype(F32)
    blank = jnp.zeros((half, LANES - 2 * size), F32)

    def rows(chunk):
        cut = slice(chunk * size, (chunk + 1) * size)
        parts = []
        for p in range(pairs):
            parts += [got[2 * p][:, cut], got[2 * p + 1][:, cut], blank]
        return jnp.concatenate(parts, axis=-1)

    query = jnp.concatenate([rows(k) for k in range(4)], axis=0).astype(BF16)
    lane = lax.broadcasted_iota(jnp.int32, (heads, width), 1)
    head = lax.broadcasted_iota(jnp.int32, (heads, width), 0)
    inner = lane % LANES
    owner = jnp.where(inner < size, 2 * (lane // LANES), 2 * (lane // LANES) + 1)
    mask = jnp.where((owner == head) & (inner < 2 * size), 1.0, 0.0).astype(F32)

    def spread(first):
        flat = jnp.concatenate([rows(first), rows(first + 1)], axis=0)
        wide = jnp.broadcast_to(flat[:, None, :], (flat.shape[0], heads, width)) * mask[None]
        return wide.reshape(flat.shape[0] * heads, width).astype(BF16)

    logits = nt_dot(query, spread(4)) * (1.0 / math.sqrt(size)) + bias_ref[...]
    slabs = logits.shape[1] // LANES

    def over_keys(values, op):
        out = functools.reduce(op, [values[:, k * LANES : (k + 1) * LANES] for k in range(slabs)])
        step = heads
        while step < LANES:
            out = op(out, pltpu.roll(out, step, 1))
            step *= 2
        return out

    peak = over_keys(logits, jnp.maximum)
    peak_hi = rounded(peak)
    peak_lo = rounded(peak - peak_hi)
    expo = jnp.exp(logits - jnp.concatenate([peak_hi + peak_lo] * slabs, axis=-1))
    denom = over_keys(expo, jnp.add)
    denom_hi = rounded(denom)
    denom_lo = rounded(denom - denom_hi)
    part = jnp.dot((expo * gate_ref[...]).astype(BF16), spread(6), preferred_element_type=F32)
    at = lax.broadcasted_iota(jnp.int32, peak.shape, 1) // heads
    stats = jnp.where(at == 0, peak_hi, jnp.where(at == 1, peak_lo, jnp.where(at == 2, denom_hi, denom_lo)))
    stats = jnp.where(at < 4, stats, 0.0).astype(BF16)
    parcel = (part + jnp.dot(stats, select_ref[...], preferred_element_type=F32)).astype(BF16)
    groups = parcel.shape[0] // half
    for g in range(groups):
        for p in range(pairs):
            parcel_ref[g * pairs + p] = parcel[g * half : (g + 1) * half, p * LANES : (p + 1) * LANES]


def settle_kernel(heard_ref, out_ref, *, size):
    heard = heard_ref[...].astype(F32)
    base = 2 * size
    lane = lax.broadcasted_iota(jnp.int32, heard.shape[1:], 1)

    def stat(which, head):
        at = base + 2 * which + head
        return heard[:, :, at : at + 1]

    mixed = None
    factors, totals = [], []
    for head in range(2):
        peaks = stat(0, head) + stat(1, head)
        factor = jnp.exp(peaks - jnp.max(peaks, axis=0, keepdims=True))
        totals.append(jnp.sum(factor * (stat(2, head) + stat(3, head)), axis=0))
        factors.append(factor)
    first = (lane < size)[None]
    factor = jnp.where(first, factors[0], factors[1])
    mixed = jnp.sum(heard * factor, axis=0)
    total = jnp.where(lane < size, totals[0], totals[1])
    attended = jnp.where(lane < base, mixed / total, 0.0).astype(BF16)
    out_ref[...] = jnp.broadcast_to(attended[None], out_ref.shape)


def output_kernel(all_ref, w_ref, out_ref, *, pairs):
    groups = all_ref.shape[0] // pairs
    whole = jnp.concatenate(
        [jnp.concatenate([all_ref[g * pairs + p] for p in range(pairs)], axis=-1) for g in range(groups)], axis=0
    )
    out_ref[...] = nt_dot(w_ref[...], whole).astype(BF16)


def mlp_kernel(odd_ref, zed_ref, pair_ref, *refs):
    backs, (w_in_ref, b_in_ref, w_out_ref, b_out_ref, out_ref, here_ref) = refs[:4], refs[4:]
    for k in range(4):

        @pl.when(pl.program_id(0) == k)
        def _():
            here_ref[...] = backs[k][...]

    width = zed_ref.shape[2]
    joined = jnp.concatenate(
        [zed_ref[...].reshape(-1, width), here_ref[...].reshape(-1, width)], axis=-1
    )
    hidden = jax.nn.gelu(jnp.dot(joined, w_in_ref[...], preferred_element_type=F32) + b_in_ref[...]).astype(BF16)
    update = jnp.dot(hidden, w_out_ref[...], preferred_element_type=F32) + b_out_ref[...]
    out_ref[...] = (pair_ref[...].astype(F32) + update.reshape(pair_ref.shape)).astype(BF16)


def whole(kernel, out_shape, flops=1 << 20, moved=1 << 18):
    return pl.pallas_call(
        kernel, out_shape=out_shape,
        compiler_params=pltpu.CompilerParams(vmem_limit_bytes=VMEM_BYTES),
        cost_estimate=pl.CostEstimate(flops=flops, bytes_accessed=moved, transcendentals=0),
    )


PIECES = (("a", 0), ("a", 1), ("b", 0), ("b", 1))


def body(
    nodes, node_gain, w_qkv, w_out, pair, pair_gain, w_bias, w_gate, b_gate, w_in, b_in, w_mlp_out, b_out,
):
    rows_n = lax.axis_size("row")
    cols_n = lax.axis_size("col")
    key_rows, node_width = nodes.shape
    row_rows, key_cols, pair_width = pair.shape
    heads = w_bias.shape[1]
    size = node_width // heads
    half = key_rows // 2
    pairs = heads // 2
    hidden_width = w_in.shape[1]
    odd = lax.axis_index("col") % 2
    ends = [(r * cols_n + c, (c // 2) * cols_n + 2 * r) for r in range(rows_n) for c in range(cols_n)]
    same = [(source, base + source % 2) for source, base in ends]
    swap = [(source, base + 1 - source % 2) for source, base in ends]

    spread, own = whole(
        project_kernel,
        (
            jax.ShapeDtypeStruct((cols_n, half, 2 * size), BF16),
            jax.ShapeDtypeStruct((2, half, 2 * size), BF16),
        ),
    )(nodes, node_gain[None], jnp.transpose(w_qkv, (0, 2, 1)))
    all_q = lax.all_to_all(spread, "col", 0, 0, tiled=True)

    zed = layer_norm(tie(pair, own), pair_gain).astype(BF16)
    landed = []
    for which, part in PIECES:
        mine = odd if which == "a" else 1 - odd
        rows = key_cols // 2
        tile = lax.dynamic_slice_in_dim(zed, mine * key_cols, key_cols, 0)[:, part * rows : (part + 1) * rows]
        landed.append(lax.ppermute(jnp.transpose(tile, (1, 0, 2)), LONG, same if which == "a" else swap))

    blocks = all_q.reshape(rows_n, 2, half, 2 * size)
    mine = [jnp.broadcast_to(own[k][None], (rows_n, half, 2 * size)) for k in range(2)]
    sent = jnp.concatenate([blocks[:, 0], blocks[:, 1]] + mine, axis=-1)
    got = lax.all_to_all(sent, "row", 0, 0, tiled=True)

    pair_bias = jnp.einsum("ijc,ch->ijh", pair, w_bias, preferred_element_type=F32)
    gate_prob = jax.nn.sigmoid(jnp.einsum("ijc,ch->ijh", zed, w_gate, preferred_element_type=F32) + b_gate)
    flat = (row_rows, key_cols * heads)
    pair_bias, gate_prob = pair_bias.reshape(flat), gate_prob.reshape(flat)

    stat = jnp.arange(LANES)[:, None]
    place = jnp.arange(pairs * LANES)[None]
    target = (stat % heads) // 2 * LANES + 2 * size + 2 * (stat // heads) + stat % 2
    select = ((place == target) & (stat < 4 * heads)).astype(BF16)
    parcel = whole(
        functools.partial(attend_kernel, heads=heads, size=size),
        jax.ShapeDtypeStruct((cols_n, row_rows * pairs // cols_n, LANES), BF16),
    )(got, pair_bias, gate_prob, select)
    heard = lax.all_to_all(parcel, "col", 0, 0, tiled=True)
    settled = whole(functools.partial(settle_kernel, size=size), jax.ShapeDtypeStruct(parcel.shape, BF16))(heard)
    everyone = lax.all_to_all(settled, "col", 0, 0, tiled=True)

    w_wide = jnp.pad(
        w_out.T.reshape(w_out.shape[1], pairs, 2 * size), ((0, 0), (0, 0), (0, LANES - 2 * size))
    ).reshape(w_out.shape[1], pairs * LANES)
    node_update = whole(
        functools.partial(output_kernel, pairs=pairs), jax.ShapeDtypeStruct((w_out.shape[1], row_rows), BF16)
    )(everyone, w_wide).T

    landed = [tie(back, settled) for back in landed]
    block = key_cols // 2

    def tile_at(k, odd_ref):
        return (jnp.where(k < 2, odd_ref[0], 1 - odd_ref[0]) * 2 + k % 2, 0, 0)

    def fixed(*shape):
        return pl.BlockSpec(shape, lambda k, odd_ref: (0,) * len(shape))

    tile_spec = pl.BlockSpec((block, key_cols, pair_width), tile_at)
    pair_out = pl.pallas_call(
        mlp_kernel,
        name="mlp",
        compiler_params=pltpu.CompilerParams(vmem_limit_bytes=VMEM_BYTES),
        grid_spec=pltpu.PrefetchScalarGridSpec(
            num_scalar_prefetch=1,
            grid=(4,),
            in_specs=[tile_spec, tile_spec]
            + [fixed(block, key_cols, pair_width)] * 4
            + [fixed(2 * pair_width, hidden_width), fixed(1, hidden_width)]
            + [fixed(hidden_width, pair_width), fixed(1, pair_width)],
            out_specs=tile_spec,
            scratch_shapes=[pltpu.VMEM((block, key_cols, pair_width), BF16)],
        ),
        out_shape=jax.ShapeDtypeStruct(pair.shape, BF16),
        cost_estimate=pl.CostEstimate(flops=8 << 26, bytes_accessed=2 << 20, transcendentals=1 << 20),
    )(odd.astype(jnp.int32)[None], zed, pair, *landed, w_in, b_in[None], w_mlp_out, b_out[None])
    return (node_update, pair_out)


def solution(mesh):
    return jax.shard_map(
        body,
        mesh=mesh,
        in_specs=(
            P("col", None), P(), P(None, None, "row"), P(None, "col"), P("row", "col", None),
            P(), P(), P(), P(), P(), P(), P(), P(),
        ),
        out_specs=(P("row", "col"), P("row", "col", None)),
        check_vma=False,
    )
```

```python
import functools
import math

import jax
import jax.numpy as jnp
from jax import lax
from jax.experimental import pallas as pl
from jax.experimental.pallas import tpu as pltpu
from jax.sharding import PartitionSpec as P

F32 = jnp.float32
BF16 = jnp.bfloat16
LONG = ("row", "col")
LANES = 128
VMEM_BYTES = 20 << 20
PROJECT_BYTES = 60 << 20


def tie(value, *others):
    return lax.optimization_barrier((value,) + others)[0]


def layer_norm(values_in, scale_gain):
    centred = values_in.astype(F32)
    centred = centred - jnp.mean(centred, axis=-1, keepdims=True)
    variance = jnp.mean(centred * centred, axis=-1, keepdims=True)
    return centred * lax.rsqrt(variance + 1e-05) * scale_gain


def nt_dot(left, right):
    return lax.dot_general(left, right, (((1,), (1,)), ((), ())), preferred_element_type=F32)


def rounded(values):
    return values.astype(BF16).astype(F32)


def project_kernel(nodes_hbm, gain_hbm, w_hbm, spread_ref, own_ref, nodes, gain, w, sems):
    copies = [
        pltpu.make_async_copy(source, target, sems.at[k])
        for k, (source, target) in enumerate(((nodes_hbm, nodes), (gain_hbm, gain), (w_hbm, w)))
    ]
    for copy in copies:
        copy.start()
    for copy in copies[:2]:
        copy.wait()
    normed = layer_norm(nodes[...], gain[...]).astype(BF16)
    half = normed.shape[0] // 2
    copies[2].wait()
    for which in range(3):
        proj = nt_dot(normed, w[which])
        packed = jnp.concatenate([proj[:half], proj[half:]], axis=-1).astype(BF16)
        if which == 0:
            spread_ref[...] = jnp.broadcast_to(packed[None], spread_ref.shape)
        else:
            own_ref[which - 1] = packed


def attend_kernel(got_ref, bias_ref, gate_ref, select_ref, parcel_ref, *, heads, size):
    half = got_ref.shape[1]
    pairs = heads // 2
    width = pairs * LANES
    got = got_ref[...].astype(F32)
    blank = jnp.zeros((half, LANES - 2 * size), F32)

    def rows(chunk):
        cut = slice(chunk * size, (chunk + 1) * size)
        parts = []
        for p in range(pairs):
            parts += [got[2 * p][:, cut], got[2 * p + 1][:, cut], blank]
        return jnp.concatenate(parts, axis=-1)

    query = jnp.concatenate([rows(k) for k in range(4)], axis=0).astype(BF16)
    lane = lax.broadcasted_iota(jnp.int32, (heads, width), 1)
    head = lax.broadcasted_iota(jnp.int32, (heads, width), 0)
    inner = lane % LANES
    owner = jnp.where(inner < size, 2 * (lane // LANES), 2 * (lane // LANES) + 1)
    mask = jnp.where((owner == head) & (inner < 2 * size), 1.0, 0.0).astype(F32)

    def spread(first):
        flat = jnp.concatenate([rows(first), rows(first + 1)], axis=0)
        wide = jnp.broadcast_to(flat[:, None, :], (flat.shape[0], heads, width)) * mask[None]
        return wide.reshape(flat.shape[0] * heads, width).astype(BF16)

    logits = nt_dot(query, spread(4)) * (1.0 / math.sqrt(size)) + bias_ref[...]
    slabs = logits.shape[1] // LANES

    def over_keys(values, op):
        out = functools.reduce(op, [values[:, k * LANES : (k + 1) * LANES] for k in range(slabs)])
        step = heads
        while step < LANES:
            out = op(out, pltpu.roll(out, step, 1))
            step *= 2
        return out

    peak = over_keys(logits, jnp.maximum)
    peak_hi = rounded(peak)
    peak_lo = rounded(peak - peak_hi)
    expo = jnp.exp(logits - jnp.concatenate([peak_hi + peak_lo] * slabs, axis=-1))
    denom = over_keys(expo, jnp.add)
    denom_hi = rounded(denom)
    denom_lo = rounded(denom - denom_hi)
    part = jnp.dot((expo * gate_ref[...]).astype(BF16), spread(6), preferred_element_type=F32)
    at = lax.broadcasted_iota(jnp.int32, peak.shape, 1) // heads
    stats = jnp.where(at == 0, peak_hi, jnp.where(at == 1, peak_lo, jnp.where(at == 2, denom_hi, denom_lo)))
    stats = jnp.where(at < 4, stats, 0.0).astype(BF16)
    parcel = (part + jnp.dot(stats, select_ref[...], preferred_element_type=F32)).astype(BF16)
    groups = parcel.shape[0] // half
    for g in range(groups):
        for p in range(pairs):
            parcel_ref[g * pairs + p] = parcel[g * half : (g + 1) * half, p * LANES : (p + 1) * LANES]


def settle_kernel(heard_ref, out_ref, *, size):
    heard = heard_ref[...].astype(F32)
    base = 2 * size
    lane = lax.broadcasted_iota(jnp.int32, heard.shape[1:], 1)

    def stat(which, head):
        at = base + 2 * which + head
        return heard[:, :, at : at + 1]

    mixed = None
    factors, totals = [], []
    for head in range(2):
        peaks = stat(0, head) + stat(1, head)
        factor = jnp.exp(peaks - jnp.max(peaks, axis=0, keepdims=True))
        totals.append(jnp.sum(factor * (stat(2, head) + stat(3, head)), axis=0))
        factors.append(factor)
    first = (lane < size)[None]
    factor = jnp.where(first, factors[0], factors[1])
    mixed = jnp.sum(heard * factor, axis=0)
    total = jnp.where(lane < size, totals[0], totals[1])
    attended = jnp.where(lane < base, mixed / total, 0.0).astype(BF16)
    out_ref[...] = jnp.broadcast_to(attended[None], out_ref.shape)


def output_kernel(all_ref, w_ref, out_ref, *, pairs):
    groups = all_ref.shape[0] // pairs
    whole = jnp.concatenate(
        [jnp.concatenate([all_ref[g * pairs + p] for p in range(pairs)], axis=-1) for g in range(groups)], axis=0
    )
    out_ref[...] = nt_dot(w_ref[...], whole).astype(BF16)


def mlp_kernel(odd_ref, zed_ref, pair_ref, *refs):
    backs, (w_in_ref, b_in_ref, w_out_ref, b_out_ref, out_ref, here_ref) = refs[:4], refs[4:]
    for k in range(4):

        @pl.when(pl.program_id(0) == k)
        def _():
            here_ref[...] = backs[k][...]

    width = zed_ref.shape[2]
    joined = jnp.concatenate(
        [zed_ref[...].reshape(-1, width), here_ref[...].reshape(-1, width)], axis=-1
    )
    hidden = jax.nn.gelu(jnp.dot(joined, w_in_ref[...], preferred_element_type=F32) + b_in_ref[...]).astype(BF16)
    update = jnp.dot(hidden, w_out_ref[...], preferred_element_type=F32) + b_out_ref[...]
    out_ref[...] = (pair_ref[...].astype(F32) + update.reshape(pair_ref.shape)).astype(BF16)


def whole(kernel, out_shape, flops=1 << 20, moved=1 << 18):
    return pl.pallas_call(
        kernel, out_shape=out_shape,
        compiler_params=pltpu.CompilerParams(vmem_limit_bytes=VMEM_BYTES),
        cost_estimate=pl.CostEstimate(flops=flops, bytes_accessed=moved, transcendentals=0),
    )


PIECES = (("a", 0), ("a", 1), ("b", 0), ("b", 1))


def body(
    nodes, node_gain, w_qkv, w_out, pair, pair_gain, w_bias, w_gate, b_gate, w_in, b_in, w_mlp_out, b_out,
):
    rows_n = lax.axis_size("row")
    cols_n = lax.axis_size("col")
    key_rows, node_width = nodes.shape
    row_rows, key_cols, pair_width = pair.shape
    heads = w_bias.shape[1]
    size = node_width // heads
    half = key_rows // 2
    pairs = heads // 2
    hidden_width = w_in.shape[1]
    odd = lax.axis_index("col") % 2
    ends = [(r * cols_n + c, (c // 2) * cols_n + 2 * r) for r in range(rows_n) for c in range(cols_n)]
    same = [(source, base + source % 2) for source, base in ends]
    swap = [(source, base + 1 - source % 2) for source, base in ends]

    hbm = pl.BlockSpec(memory_space=pltpu.MemorySpace.HBM)
    spread, own = pl.pallas_call(
        project_kernel,
        name="project",
        compiler_params=pltpu.CompilerParams(vmem_limit_bytes=PROJECT_BYTES),
        in_specs=[hbm] * 3,
        out_shape=(
            jax.ShapeDtypeStruct((cols_n, half, 2 * size), BF16),
            jax.ShapeDtypeStruct((2, half, 2 * size), BF16),
        ),
        scratch_shapes=[
            pltpu.VMEM(nodes.shape, BF16),
            pltpu.VMEM(node_gain.shape, F32),
            pltpu.VMEM((3, size, node_width), BF16),
            pltpu.SemaphoreType.DMA((3,)),
        ],
    )(nodes, node_gain, jnp.transpose(w_qkv, (0, 2, 1)))
    all_q = lax.all_to_all(spread, "col", 0, 0, tiled=True)

    zed = layer_norm(tie(pair, own), pair_gain).astype(BF16)
    landed = []
    for which, part in PIECES:
        mine = odd if which == "a" else 1 - odd
        rows = key_cols // 2
        tile = lax.dynamic_slice_in_dim(zed, mine * key_cols, key_cols, 0)[:, part * rows : (part + 1) * rows]
        landed.append(lax.ppermute(jnp.transpose(tile, (1, 0, 2)), LONG, same if which == "a" else swap))

    blocks = all_q.reshape(rows_n, 2, half, 2 * size)
    mine = [jnp.broadcast_to(own[k][None], (rows_n, half, 2 * size)) for k in range(2)]
    sent = jnp.concatenate([blocks[:, 0], blocks[:, 1]] + mine, axis=-1)
    got = lax.all_to_all(sent, "row", 0, 0, tiled=True)

    pair_bias = jnp.einsum("ijc,ch->ijh", pair, w_bias, preferred_element_type=F32)
    gate_prob = jax.nn.sigmoid(jnp.einsum("ijc,ch->ijh", zed, w_gate, preferred_element_type=F32) + b_gate)
    flat = (row_rows, key_cols * heads)
    pair_bias, gate_prob = pair_bias.reshape(flat), gate_prob.reshape(flat)

    stat = jnp.arange(LANES)[:, None]
    place = jnp.arange(pairs * LANES)[None]
    target = (stat % heads) // 2 * LANES + 2 * size + 2 * (stat // heads) + stat % 2
    select = ((place == target) & (stat < 4 * heads)).astype(BF16)
    parcel = whole(
        functools.partial(attend_kernel, heads=heads, size=size),
        jax.ShapeDtypeStruct((cols_n, row_rows * pairs // cols_n, LANES), BF16),
    )(got, pair_bias, gate_prob, select)
    heard = lax.all_to_all(parcel, "col", 0, 0, tiled=True)
    settled = whole(functools.partial(settle_kernel, size=size), jax.ShapeDtypeStruct(parcel.shape, BF16))(heard)
    everyone = lax.all_to_all(settled, "col", 0, 0, tiled=True)

    w_wide = jnp.pad(
        w_out.T.reshape(w_out.shape[1], pairs, 2 * size), ((0, 0), (0, 0), (0, LANES - 2 * size))
    ).reshape(w_out.shape[1], pairs * LANES)
    node_update = whole(
        functools.partial(output_kernel, pairs=pairs), jax.ShapeDtypeStruct((w_out.shape[1], row_rows), BF16)
    )(everyone, w_wide).T

    landed = [tie(back, settled) for back in landed]
    block = key_cols // 2

    def tile_at(k, odd_ref):
        return (jnp.where(k < 2, odd_ref[0], 1 - odd_ref[0]) * 2 + k % 2, 0, 0)

    def fixed(*shape):
        return pl.BlockSpec(shape, lambda k, odd_ref: (0,) * len(shape))

    tile_spec = pl.BlockSpec((block, key_cols, pair_width), tile_at)
    pair_out = pl.pallas_call(
        mlp_kernel,
        name="mlp",
        compiler_params=pltpu.CompilerParams(vmem_limit_bytes=VMEM_BYTES),
        grid_spec=pltpu.PrefetchScalarGridSpec(
            num_scalar_prefetch=1,
            grid=(4,),
            in_specs=[tile_spec, tile_spec]
            + [fixed(block, key_cols, pair_width)] * 4
            + [fixed(2 * pair_width, hidden_width), fixed(1, hidden_width)]
            + [fixed(hidden_width, pair_width), fixed(1, pair_width)],
            out_specs=tile_spec,
            scratch_shapes=[pltpu.VMEM((block, key_cols, pair_width), BF16)],
        ),
        out_shape=jax.ShapeDtypeStruct(pair.shape, BF16),
        cost_estimate=pl.CostEstimate(flops=8 << 26, bytes_accessed=2 << 20, transcendentals=1 << 20),
    )(odd.astype(jnp.int32)[None], zed, pair, *landed, w_in, b_in[None], w_mlp_out, b_out[None])
    return (node_update, pair_out)


def solution(mesh):
    return jax.shard_map(
        body,
        mesh=mesh,
        in_specs=(
            P("col", None), P(), P(None, None, "row"), P(None, "col"), P("row", "col", None),
            P(), P(), P(), P(), P(), P(), P(), P(),
        ),
        out_specs=(P("row", "col"), P("row", "col", None)),
        check_vma=False,
    )
```

```python
import functools
import math

import jax
import jax.numpy as jnp
from jax import lax
from jax.experimental import pallas as pl
from jax.experimental.pallas import tpu as pltpu
from jax.sharding import PartitionSpec as P

F32 = jnp.float32
BF16 = jnp.bfloat16
LONG = ("row", "col")
LANES = 128
VMEM_BYTES = 20 << 20
PROJECT_BYTES = 60 << 20


def tie(value, *others):
    return lax.optimization_barrier((value,) + others)[0]


def layer_norm(values_in, scale_gain):
    centred = values_in.astype(F32)
    centred = centred - jnp.mean(centred, axis=-1, keepdims=True)
    variance = jnp.mean(centred * centred, axis=-1, keepdims=True)
    return centred * lax.rsqrt(variance + 1e-05) * scale_gain


def nt_dot(left, right):
    return lax.dot_general(left, right, (((1,), (1,)), ((), ())), preferred_element_type=F32)


def rounded(values):
    return values.astype(BF16).astype(F32)


def project_kernel(nodes_hbm, gain_hbm, w_hbm, spread_ref, own_ref, nodes, gain, w, sems):
    copies = [
        pltpu.make_async_copy(source, target, sems.at[k])
        for k, (source, target) in enumerate(((nodes_hbm, nodes), (gain_hbm, gain), (w_hbm, w)))
    ]
    for copy in copies:
        copy.start()
    for copy in copies[:2]:
        copy.wait()
    normed = layer_norm(nodes[...], gain[...]).astype(BF16)
    half = normed.shape[0] // 2
    copies[2].wait()
    for which in range(3):
        proj = nt_dot(normed, w[which])
        packed = jnp.concatenate([proj[:half], proj[half:]], axis=-1).astype(BF16)
        if which == 0:
            spread_ref[...] = jnp.broadcast_to(packed[None], spread_ref.shape)
        else:
            own_ref[which - 1] = packed


def pack_kernel(all_ref, own_ref, out_ref):
    own = jnp.concatenate([own_ref[0].astype(F32), own_ref[1].astype(F32)], axis=-1)
    for r in range(out_ref.shape[0]):
        left, right = all_ref[2 * r].astype(F32), all_ref[2 * r + 1].astype(F32)
        out_ref[r] = jnp.concatenate([left, right, own], axis=-1).astype(BF16)


def attend_kernel(got_ref, bias_ref, gate_ref, select_ref, parcel_ref, *, heads, size):
    half = got_ref.shape[1]
    pairs = heads // 2
    width = pairs * LANES
    got = got_ref[...].astype(F32)
    blank = jnp.zeros((half, LANES - 2 * size), F32)

    def rows(chunk):
        cut = slice(chunk * size, (chunk + 1) * size)
        parts = []
        for p in range(pairs):
            parts += [got[2 * p][:, cut], got[2 * p + 1][:, cut], blank]
        return jnp.concatenate(parts, axis=-1)

    query = jnp.concatenate([rows(k) for k in range(4)], axis=0).astype(BF16)
    lane = lax.broadcasted_iota(jnp.int32, (heads, width), 1)
    head = lax.broadcasted_iota(jnp.int32, (heads, width), 0)
    inner = lane % LANES
    owner = jnp.where(inner < size, 2 * (lane // LANES), 2 * (lane // LANES) + 1)
    mask = jnp.where((owner == head) & (inner < 2 * size), 1.0, 0.0).astype(F32)

    def spread(first):
        flat = jnp.concatenate([rows(first), rows(first + 1)], axis=0)
        wide = jnp.broadcast_to(flat[:, None, :], (flat.shape[0], heads, width)) * mask[None]
        return wide.reshape(flat.shape[0] * heads, width).astype(BF16)

    logits = nt_dot(query, spread(4)) * (1.0 / math.sqrt(size)) + bias_ref[...]
    slabs = logits.shape[1] // LANES

    def over_keys(values, op):
        out = functools.reduce(op, [values[:, k * LANES : (k + 1) * LANES] for k in range(slabs)])
        step = heads
        while step < LANES:
            out = op(out, pltpu.roll(out, step, 1))
            step *= 2
        return out

    peak = over_keys(logits, jnp.maximum)
    peak_hi = rounded(peak)
    peak_lo = rounded(peak - peak_hi)
    expo = jnp.exp(logits - jnp.concatenate([peak_hi + peak_lo] * slabs, axis=-1))
    denom = over_keys(expo, jnp.add)
    denom_hi = rounded(denom)
    denom_lo = rounded(denom - denom_hi)
    part = jnp.dot((expo * gate_ref[...]).astype(BF16), spread(6), preferred_element_type=F32)
    at = lax.broadcasted_iota(jnp.int32, peak.shape, 1) // heads
    stats = jnp.where(at == 0, peak_hi, jnp.where(at == 1, peak_lo, jnp.where(at == 2, denom_hi, denom_lo)))
    stats = jnp.where(at < 4, stats, 0.0).astype(BF16)
    parcel = (part + jnp.dot(stats, select_ref[...], preferred_element_type=F32)).astype(BF16)
    groups = parcel.shape[0] // half
    for g in range(groups):
        for p in range(pairs):
            parcel_ref[g * pairs + p] = parcel[g * half : (g + 1) * half, p * LANES : (p + 1) * LANES]


def settle_kernel(heard_ref, out_ref, *, size):
    heard = heard_ref[...].astype(F32)
    base = 2 * size
    lane = lax.broadcasted_iota(jnp.int32, heard.shape[1:], 1)

    def stat(which, head):
        at = base + 2 * which + head
        return heard[:, :, at : at + 1]

    mixed = None
    factors, totals = [], []
    for head in range(2):
        peaks = stat(0, head) + stat(1, head)
        factor = jnp.exp(peaks - jnp.max(peaks, axis=0, keepdims=True))
        totals.append(jnp.sum(factor * (stat(2, head) + stat(3, head)), axis=0))
        factors.append(factor)
    first = (lane < size)[None]
    factor = jnp.where(first, factors[0], factors[1])
    mixed = jnp.sum(heard * factor, axis=0)
    total = jnp.where(lane < size, totals[0], totals[1])
    attended = jnp.where(lane < base, mixed / total, 0.0).astype(BF16)
    out_ref[...] = jnp.broadcast_to(attended[None], out_ref.shape)


def output_kernel(all_ref, w_ref, out_ref, *, pairs):
    groups = all_ref.shape[0] // pairs
    whole = jnp.concatenate(
        [jnp.concatenate([all_ref[g * pairs + p] for p in range(pairs)], axis=-1) for g in range(groups)], axis=0
    )
    out_ref[...] = nt_dot(w_ref[...], whole).astype(BF16)


def mlp_kernel(odd_ref, zed_ref, pair_ref, *refs):
    backs, (w_in_ref, b_in_ref, w_out_ref, b_out_ref, out_ref, here_ref) = refs[:4], refs[4:]
    for k in range(4):

        @pl.when(pl.program_id(0) == k)
        def _():
            here_ref[...] = backs[k][...]

    width = zed_ref.shape[2]
    joined = jnp.concatenate(
        [zed_ref[...].reshape(-1, width), here_ref[...].reshape(-1, width)], axis=-1
    )
    hidden = jax.nn.gelu(jnp.dot(joined, w_in_ref[...], preferred_element_type=F32) + b_in_ref[...]).astype(BF16)
    update = jnp.dot(hidden, w_out_ref[...], preferred_element_type=F32) + b_out_ref[...]
    out_ref[...] = (pair_ref[...].astype(F32) + update.reshape(pair_ref.shape)).astype(BF16)


def whole(kernel, out_shape, flops=1 << 20, moved=1 << 18):
    return pl.pallas_call(
        kernel, out_shape=out_shape,
        compiler_params=pltpu.CompilerParams(vmem_limit_bytes=VMEM_BYTES),
        cost_estimate=pl.CostEstimate(flops=flops, bytes_accessed=moved, transcendentals=0),
    )


PIECES = (("a", 0), ("a", 1), ("b", 0), ("b", 1))


def body(
    nodes, node_gain, w_qkv, w_out, pair, pair_gain, w_bias, w_gate, b_gate, w_in, b_in, w_mlp_out, b_out,
):
    rows_n = lax.axis_size("row")
    cols_n = lax.axis_size("col")
    key_rows, node_width = nodes.shape
    row_rows, key_cols, pair_width = pair.shape
    heads = w_bias.shape[1]
    size = node_width // heads
    half = key_rows // 2
    pairs = heads // 2
    hidden_width = w_in.shape[1]
    odd = lax.axis_index("col") % 2
    ends = [(r * cols_n + c, (c // 2) * cols_n + 2 * r) for r in range(rows_n) for c in range(cols_n)]
    same = [(source, base + source % 2) for source, base in ends]
    swap = [(source, base + 1 - source % 2) for source, base in ends]

    hbm = pl.BlockSpec(memory_space=pltpu.MemorySpace.HBM)
    spread, own = pl.pallas_call(
        project_kernel,
        name="project",
        compiler_params=pltpu.CompilerParams(vmem_limit_bytes=PROJECT_BYTES),
        in_specs=[hbm] * 3,
        out_shape=(
            jax.ShapeDtypeStruct((cols_n, half, 2 * size), BF16),
            jax.ShapeDtypeStruct((2, half, 2 * size), BF16),
        ),
        scratch_shapes=[
            pltpu.VMEM(nodes.shape, BF16),
            pltpu.VMEM(node_gain.shape, F32),
            pltpu.VMEM((3, size, node_width), BF16),
            pltpu.SemaphoreType.DMA((3,)),
        ],
    )(nodes, node_gain, jnp.transpose(w_qkv, (0, 2, 1)))
    all_q = lax.all_to_all(spread, "col", 0, 0, tiled=True)

    zed = layer_norm(tie(pair, own), pair_gain).astype(BF16)
    landed = []
    for which, part in PIECES:
        mine = odd if which == "a" else 1 - odd
        rows = key_cols // 2
        tile = lax.dynamic_slice_in_dim(zed, mine * key_cols, key_cols, 0)[:, part * rows : (part + 1) * rows]
        landed.append(lax.ppermute(jnp.transpose(tile, (1, 0, 2)), LONG, same if which == "a" else swap))

    sent = whole(pack_kernel, jax.ShapeDtypeStruct((rows_n, half, 8 * size), BF16))(all_q, own)
    got = lax.all_to_all(sent, "row", 0, 0, tiled=True)

    pair_bias = jnp.einsum("ijc,ch->ijh", pair, w_bias, preferred_element_type=F32)
    gate_prob = jax.nn.sigmoid(jnp.einsum("ijc,ch->ijh", zed, w_gate, preferred_element_type=F32) + b_gate)
    flat = (row_rows, key_cols * heads)
    pair_bias, gate_prob = pair_bias.reshape(flat), gate_prob.reshape(flat)

    stat = jnp.arange(LANES)[:, None]
    place = jnp.arange(pairs * LANES)[None]
    target = (stat % heads) // 2 * LANES + 2 * size + 2 * (stat // heads) + stat % 2
    select = ((place == target) & (stat < 4 * heads)).astype(BF16)
    parcel = whole(
        functools.partial(attend_kernel, heads=heads, size=size),
        jax.ShapeDtypeStruct((cols_n, row_rows * pairs // cols_n, LANES), BF16),
    )(got, pair_bias, gate_prob, select)
    heard = lax.all_to_all(parcel, "col", 0, 0, tiled=True)
    settled = whole(functools.partial(settle_kernel, size=size), jax.ShapeDtypeStruct(parcel.shape, BF16))(heard)
    everyone = lax.all_to_all(settled, "col", 0, 0, tiled=True)

    w_wide = jnp.pad(
        w_out.T.reshape(w_out.shape[1], pairs, 2 * size), ((0, 0), (0, 0), (0, LANES - 2 * size))
    ).reshape(w_out.shape[1], pairs * LANES)
    node_update = whole(
        functools.partial(output_kernel, pairs=pairs), jax.ShapeDtypeStruct((w_out.shape[1], row_rows), BF16)
    )(everyone, w_wide).T

    landed = [tie(back, settled) for back in landed]
    block = key_cols // 2

    def tile_at(k, odd_ref):
        return (jnp.where(k < 2, odd_ref[0], 1 - odd_ref[0]) * 2 + k % 2, 0, 0)

    def fixed(*shape):
        return pl.BlockSpec(shape, lambda k, odd_ref: (0,) * len(shape))

    tile_spec = pl.BlockSpec((block, key_cols, pair_width), tile_at)
    pair_out = pl.pallas_call(
        mlp_kernel,
        name="mlp",
        compiler_params=pltpu.CompilerParams(vmem_limit_bytes=VMEM_BYTES),
        grid_spec=pltpu.PrefetchScalarGridSpec(
            num_scalar_prefetch=1,
            grid=(4,),
            in_specs=[tile_spec, tile_spec]
            + [fixed(block, key_cols, pair_width)] * 4
            + [fixed(2 * pair_width, hidden_width), fixed(1, hidden_width)]
            + [fixed(hidden_width, pair_width), fixed(1, pair_width)],
            out_specs=tile_spec,
            scratch_shapes=[pltpu.VMEM((block, key_cols, pair_width), BF16)],
        ),
        out_shape=jax.ShapeDtypeStruct(pair.shape, BF16),
        cost_estimate=pl.CostEstimate(flops=8 << 26, bytes_accessed=2 << 20, transcendentals=1 << 20),
    )(odd.astype(jnp.int32)[None], zed, pair, *landed, w_in, b_in[None], w_mlp_out, b_out[None])
    return (node_update, pair_out)


def solution(mesh):
    return jax.shard_map(
        body,
        mesh=mesh,
        in_specs=(
            P("col", None), P(), P(None, None, "row"), P(None, "col"), P("row", "col", None),
            P(), P(), P(), P(), P(), P(), P(), P(),
        ),
        out_specs=(P("row", "col"), P("row", "col", None)),
        check_vma=False,
    )
```

```python
import functools
import math

import jax
import jax.numpy as jnp
from jax import lax
from jax.experimental import pallas as pl
from jax.experimental.pallas import tpu as pltpu
from jax.sharding import PartitionSpec as P

F32 = jnp.float32
BF16 = jnp.bfloat16
LONG = ("row", "col")
LANES = 128
VMEM_BYTES = 20 << 20
PROJECT_BYTES = 60 << 20


def tie(value, *others):
    return lax.optimization_barrier((value,) + others)[0]


def layer_norm(values_in, scale_gain):
    centred = values_in.astype(F32)
    centred = centred - jnp.mean(centred, axis=-1, keepdims=True)
    variance = jnp.mean(centred * centred, axis=-1, keepdims=True)
    return centred * lax.rsqrt(variance + 1e-05) * scale_gain


def nt_dot(left, right):
    return lax.dot_general(left, right, (((1,), (1,)), ((), ())), preferred_element_type=F32)


def rounded(values):
    return values.astype(BF16).astype(F32)


def project_kernel(nodes_hbm, gain_hbm, w_hbm, spread_ref, own_ref, nodes, gain, w, sems):
    copies = [
        pltpu.make_async_copy(source, target, sems.at[k])
        for k, (source, target) in enumerate(((nodes_hbm, nodes), (gain_hbm, gain), (w_hbm, w)))
    ]
    for copy in copies:
        copy.start()
    for copy in copies[:2]:
        copy.wait()
    normed = layer_norm(nodes[...], gain[...]).astype(BF16)
    half = normed.shape[0] // 2
    copies[2].wait()
    for which in range(3):
        proj = nt_dot(normed, w[which])
        packed = jnp.concatenate([proj[:half], proj[half:]], axis=-1).astype(BF16)
        if which == 0:
            spread_ref[...] = jnp.broadcast_to(packed[None], spread_ref.shape)
        else:
            own_ref[which - 1] = packed


def pack_kernel(all_ref, own_ref, out_ref):
    own = jnp.concatenate([own_ref[0].astype(F32), own_ref[1].astype(F32)], axis=-1)
    for r in range(out_ref.shape[0]):
        left, right = all_ref[2 * r].astype(F32), all_ref[2 * r + 1].astype(F32)
        out_ref[r] = jnp.concatenate([left, right, own], axis=-1).astype(BF16)


def attend_kernel(got_ref, bias_ref, gate_ref, select_ref, parcel_ref, *, heads, size):
    half = got_ref.shape[1]
    pairs = heads // 2
    width = pairs * LANES
    got = got_ref[...].astype(F32)
    blank = jnp.zeros((half, LANES - 2 * size), F32)

    def rows(chunk):
        cut = slice(chunk * size, (chunk + 1) * size)
        parts = []
        for p in range(pairs):
            parts += [got[2 * p][:, cut], got[2 * p + 1][:, cut], blank]
        return jnp.concatenate(parts, axis=-1)

    query = jnp.concatenate([rows(k) for k in range(4)], axis=0).astype(BF16)
    lane = lax.broadcasted_iota(jnp.int32, (heads, width), 1)
    head = lax.broadcasted_iota(jnp.int32, (heads, width), 0)
    inner = lane % LANES
    owner = jnp.where(inner < size, 2 * (lane // LANES), 2 * (lane // LANES) + 1)
    mask = jnp.where((owner == head) & (inner < 2 * size), 1.0, 0.0).astype(F32)

    def spread(first):
        flat = jnp.concatenate([rows(first), rows(first + 1)], axis=0)
        wide = jnp.broadcast_to(flat[:, None, :], (flat.shape[0], heads, width)) * mask[None]
        return wide.reshape(flat.shape[0] * heads, width).astype(BF16)

    logits = nt_dot(query, spread(4)) * (1.0 / math.sqrt(size)) + bias_ref[...]
    slabs = logits.shape[1] // LANES

    def over_keys(values, op):
        out = functools.reduce(op, [values[:, k * LANES : (k + 1) * LANES] for k in range(slabs)])
        step = heads
        while step < LANES:
            out = op(out, pltpu.roll(out, step, 1))
            step *= 2
        return out

    peak = over_keys(logits, jnp.maximum)
    peak_hi = rounded(peak)
    peak_lo = rounded(peak - peak_hi)
    expo = jnp.exp(logits - jnp.concatenate([peak_hi + peak_lo] * slabs, axis=-1))
    denom = over_keys(expo, jnp.add)
    denom_hi = rounded(denom)
    denom_lo = rounded(denom - denom_hi)
    part = jnp.dot((expo * gate_ref[...]).astype(BF16), spread(6), preferred_element_type=F32)
    at = lax.broadcasted_iota(jnp.int32, peak.shape, 1) // heads
    stats = jnp.where(at == 0, peak_hi, jnp.where(at == 1, peak_lo, jnp.where(at == 2, denom_hi, denom_lo)))
    stats = jnp.where(at < 4, stats, 0.0).astype(BF16)
    parcel = (part + jnp.dot(stats, select_ref[...], preferred_element_type=F32)).astype(BF16)
    groups = parcel.shape[0] // half
    for g in range(groups):
        for p in range(pairs):
            parcel_ref[g * pairs + p] = parcel[g * half : (g + 1) * half, p * LANES : (p + 1) * LANES]


def settle_kernel(heard_ref, out_ref, *, size):
    heard = heard_ref[...].astype(F32)
    base = 2 * size
    lane = lax.broadcasted_iota(jnp.int32, heard.shape[1:], 1)

    def stat(which, head):
        at = base + 2 * which + head
        return heard[:, :, at : at + 1]

    mixed = None
    factors, totals = [], []
    for head in range(2):
        peaks = stat(0, head) + stat(1, head)
        factor = jnp.exp(peaks - jnp.max(peaks, axis=0, keepdims=True))
        totals.append(jnp.sum(factor * (stat(2, head) + stat(3, head)), axis=0))
        factors.append(factor)
    first = (lane < size)[None]
    factor = jnp.where(first, factors[0], factors[1])
    mixed = jnp.sum(heard * factor, axis=0)
    total = jnp.where(lane < size, totals[0], totals[1])
    attended = jnp.where(lane < base, mixed / total, 0.0).astype(BF16)
    out_ref[...] = jnp.broadcast_to(attended[None], out_ref.shape)


def output_kernel(all_ref, w_ref, out_ref, *, pairs):
    groups = all_ref.shape[0] // pairs
    whole = jnp.concatenate(
        [jnp.concatenate([all_ref[g * pairs + p] for p in range(pairs)], axis=-1) for g in range(groups)], axis=0
    )
    out_ref[...] = nt_dot(w_ref[...], whole).astype(BF16)


def mlp_kernel(odd_ref, zed_ref, pair_ref, *refs):
    backs, (w_in_ref, b_in_ref, w_out_ref, b_out_ref, out_ref, here_ref) = refs[:4], refs[4:]
    for k in range(4):

        @pl.when(pl.program_id(0) == k)
        def _():
            here_ref[...] = backs[k][...]

    width = zed_ref.shape[2]
    joined = jnp.concatenate(
        [zed_ref[...].reshape(-1, width), here_ref[...].reshape(-1, width)], axis=-1
    )
    hidden = jax.nn.gelu(jnp.dot(joined, w_in_ref[...], preferred_element_type=F32) + b_in_ref[...]).astype(BF16)
    update = jnp.dot(hidden, w_out_ref[...], preferred_element_type=F32) + b_out_ref[...]
    out_ref[...] = (pair_ref[...].astype(F32) + update.reshape(pair_ref.shape)).astype(BF16)


def whole(kernel, out_shape, flops=1 << 20, moved=1 << 18):
    return pl.pallas_call(
        kernel, out_shape=out_shape,
        compiler_params=pltpu.CompilerParams(vmem_limit_bytes=VMEM_BYTES),
        cost_estimate=pl.CostEstimate(flops=flops, bytes_accessed=moved, transcendentals=0),
    )


PIECES = (("a", 0), ("a", 1), ("b", 0), ("b", 1))


def body(
    nodes, node_gain, w_qkv, w_out, pair, pair_gain, w_bias, w_gate, b_gate, w_in, b_in, w_mlp_out, b_out,
):
    rows_n = lax.axis_size("row")
    cols_n = lax.axis_size("col")
    key_rows, node_width = nodes.shape
    row_rows, key_cols, pair_width = pair.shape
    heads = w_bias.shape[1]
    size = node_width // heads
    half = key_rows // 2
    pairs = heads // 2
    hidden_width = w_in.shape[1]
    odd = lax.axis_index("col") % 2
    ends = [(r * cols_n + c, (c // 2) * cols_n + 2 * r) for r in range(rows_n) for c in range(cols_n)]
    same = [(source, base + source % 2) for source, base in ends]
    swap = [(source, base + 1 - source % 2) for source, base in ends]

    hbm = pl.BlockSpec(memory_space=pltpu.MemorySpace.HBM)
    spread, own = pl.pallas_call(
        project_kernel,
        name="project",
        compiler_params=pltpu.CompilerParams(vmem_limit_bytes=PROJECT_BYTES),
        in_specs=[hbm] * 3,
        out_shape=(
            jax.ShapeDtypeStruct((cols_n, half, 2 * size), BF16),
            jax.ShapeDtypeStruct((2, half, 2 * size), BF16),
        ),
        scratch_shapes=[
            pltpu.VMEM(nodes.shape, BF16),
            pltpu.VMEM(node_gain.shape, F32),
            pltpu.VMEM((3, size, node_width), BF16),
            pltpu.SemaphoreType.DMA((3,)),
        ],
    )(nodes, node_gain, jnp.transpose(w_qkv, (0, 2, 1)))
    all_q = lax.all_to_all(spread, "col", 0, 0, tiled=True)

    landed = []
    for index, (which, part) in enumerate(PIECES):
        mine = odd if which == "a" else 1 - odd
        rows = key_cols // 2
        if index:
            tile = lax.dynamic_slice_in_dim(zed, mine * key_cols, key_cols, 0)[:, part * rows : (part + 1) * rows]
        else:
            raw = lax.dynamic_slice_in_dim(pair, mine * key_cols, key_cols, 0)[:, part * rows : (part + 1) * rows]
            tile = layer_norm(tie(raw, own), pair_gain).astype(BF16)
            zed = layer_norm(tie(pair, tile), pair_gain).astype(BF16)
        landed.append(lax.ppermute(jnp.transpose(tile, (1, 0, 2)), LONG, same if which == "a" else swap))

    sent = whole(pack_kernel, jax.ShapeDtypeStruct((rows_n, half, 8 * size), BF16))(all_q, own)
    got = lax.all_to_all(sent, "row", 0, 0, tiled=True)

    pair_bias = jnp.einsum("ijc,ch->ijh", pair, w_bias, preferred_element_type=F32)
    gate_prob = jax.nn.sigmoid(jnp.einsum("ijc,ch->ijh", zed, w_gate, preferred_element_type=F32) + b_gate)
    flat = (row_rows, key_cols * heads)
    pair_bias, gate_prob = pair_bias.reshape(flat), gate_prob.reshape(flat)

    stat = jnp.arange(LANES)[:, None]
    place = jnp.arange(pairs * LANES)[None]
    target = (stat % heads) // 2 * LANES + 2 * size + 2 * (stat // heads) + stat % 2
    select = ((place == target) & (stat < 4 * heads)).astype(BF16)
    parcel = whole(
        functools.partial(attend_kernel, heads=heads, size=size),
        jax.ShapeDtypeStruct((cols_n, row_rows * pairs // cols_n, LANES), BF16),
    )(got, pair_bias, gate_prob, select)
    heard = lax.all_to_all(parcel, "col", 0, 0, tiled=True)
    settled = whole(functools.partial(settle_kernel, size=size), jax.ShapeDtypeStruct(parcel.shape, BF16))(heard)
    everyone = lax.all_to_all(settled, "col", 0, 0, tiled=True)

    w_wide = jnp.pad(
        w_out.T.reshape(w_out.shape[1], pairs, 2 * size), ((0, 0), (0, 0), (0, LANES - 2 * size))
    ).reshape(w_out.shape[1], pairs * LANES)
    node_update = whole(
        functools.partial(output_kernel, pairs=pairs), jax.ShapeDtypeStruct((w_out.shape[1], row_rows), BF16)
    )(everyone, w_wide).T

    landed = [tie(back, settled) for back in landed]
    block = key_cols // 2

    def tile_at(k, odd_ref):
        return (jnp.where(k < 2, odd_ref[0], 1 - odd_ref[0]) * 2 + k % 2, 0, 0)

    def fixed(*shape):
        return pl.BlockSpec(shape, lambda k, odd_ref: (0,) * len(shape))

    tile_spec = pl.BlockSpec((block, key_cols, pair_width), tile_at)
    pair_out = pl.pallas_call(
        mlp_kernel,
        name="mlp",
        compiler_params=pltpu.CompilerParams(vmem_limit_bytes=VMEM_BYTES),
        grid_spec=pltpu.PrefetchScalarGridSpec(
            num_scalar_prefetch=1,
            grid=(4,),
            in_specs=[tile_spec, tile_spec]
            + [fixed(block, key_cols, pair_width)] * 4
            + [fixed(2 * pair_width, hidden_width), fixed(1, hidden_width)]
            + [fixed(hidden_width, pair_width), fixed(1, pair_width)],
            out_specs=tile_spec,
            scratch_shapes=[pltpu.VMEM((block, key_cols, pair_width), BF16)],
        ),
        out_shape=jax.ShapeDtypeStruct(pair.shape, BF16),
        cost_estimate=pl.CostEstimate(flops=8 << 26, bytes_accessed=2 << 20, transcendentals=1 << 20),
    )(odd.astype(jnp.int32)[None], zed, pair, *landed, w_in, b_in[None], w_mlp_out, b_out[None])
    return (node_update, pair_out)


def solution(mesh):
    return jax.shard_map(
        body,
        mesh=mesh,
        in_specs=(
            P("col", None), P(), P(None, None, "row"), P(None, "col"), P("row", "col", None),
            P(), P(), P(), P(), P(), P(), P(), P(),
        ),
        out_specs=(P("row", "col"), P("row", "col", None)),
        check_vma=False,
    )
```
